32 devices in a mesh: seq: 8 (over z, core), chan: 4 (over y, x).
Axes of the slice: x: 2, y: 2, z: 4, core: 2. Of those that a mesh axis runs over, the one named last changes fastest.
Arguments:
- query_proj: bfloat16 [1024, 16384], P('chan', 'seq'), may hold values from -6 to 6
- key_proj: bfloat16 [1024, 16384], P('chan', 'seq'), may hold values from -6 to 6
- value_proj: bfloat16 [1024, 16384], P('chan', 'seq'), may hold values from -6 to 6
- short_taps: bfloat16 [3, 7, 1024], P(None, None, 'chan'), may hold values from -2 to 2
- skip_gain: float32 [1024], P('chan'), may hold values from 0.5 to 1.5
- filter_raw: bfloat16 [1024, 16384], P(None, ('seq', 'chan')), may hold values from -6 to 6
- grad_out: bfloat16 [1024, 16384], P('chan', 'seq'), may hold values from -6 to 6
Outputs:
- mixed_out: bfloat16 [1024, 16384], P('chan', 'seq')
- grad_query: bfloat16 [1024, 16384], P('chan', 'seq')
- grad_key: bfloat16 [1024, 16384], P('chan', 'seq')
- grad_value: bfloat16 [1024, 16384], P('chan', 'seq')
- grad_short: float32 [3, 7, 1024], P(None, None, 'chan')
- grad_skip: float32 [1024], P('chan')
- grad_filter: bfloat16 [1024, 16384], P(None, ('seq', 'chan'))
The draws below stay inside these ranges and needn't reach their ends.
All inputs are finite; a program needn't handle non-finite values.
Results may differ from the reference program's by a relative error of at most 0.013.
Values may be sent and summed in bfloat16 or wider, within the bound.
A program may use at most 192 MiB of HBM per device.

```python
import math
import jax
import jax.numpy as jnp
from jax import lax

C = 1024
SHORT = 7
L = 16384


def steps_of(key, extent, cuts, smallest, top_value):
    loudness, own = 1.0, jax.random.fold_in(key, 6)
    for axis_at, parts in cuts:
        heights = jnp.exp(jax.random.uniform(jax.random.fold_in(own, axis_at), (parts,), jnp.float32, smallest / len(cuts), top_value / len(cuts)))
        loudness = loudness * jnp.repeat(heights, extent[axis_at] // parts).reshape([-1 if axis == axis_at else 1 for axis in range(len(extent))])
    return loudness


def noise(own_key, extent, width, most, split=(), held_as=jnp.bfloat16):
    array = jax.random.normal(own_key, extent, jnp.float32) * width
    if len(split) > 0:
        array = steps_of(own_key, extent, split, -0.22, 0.18) * array
    return jnp.clip(array, min=-most, max=most).astype(held_as)


def setup_inputs(seed: int = 0) -> dict:
    splits = jax.random.split(jax.random.key(seed), 8)
    return {
        "query_proj": noise(splits[0], (C, L), 1.0, 6.0, ((0, 4), (1, 8))),
        "key_proj": noise(splits[1], (C, L), 1.0, 6.0, ((0, 4), (1, 8))),
        "value_proj": noise(splits[2], (C, L), 1.0, 6.0, ((0, 4), (1, 8))),
        "short_taps": noise(splits[3], (3, SHORT, C), SHORT ** -0.5, 2.0, ((2, 4),)),
        "skip_gain": jnp.clip(0.5 + 1.0 * jax.random.uniform(splits[4], (C,), jnp.float32) ** steps_of(splits[4], (C,), ((0, 4),), -0.2, 0.2), 0.5, 1.5),
        "filter_raw": noise(splits[5], (C, L), 1.0, 6.0, ((1, 32),)),
        "grad_out": noise(splits[6], (C, L), 1.0, 6.0, ((0, 4), (1, 8))),
    }


def short_causal(padded, taps):
    span = taps.shape[1]
    length = padded.shape[-1] - (span - 1)
    running = jnp.zeros(padded.shape[:-1] + (length,), jnp.float32)
    for offset in range(span):
        begin_at = span - 1 - offset
        running = running + taps[:, offset, :, None].astype(jnp.float32) * padded[..., begin_at:begin_at + length].astype(jnp.float32)
    return running

def short_anticausal(padded, taps):
    span = taps.shape[1]
    length = padded.shape[-1] - (span - 1)
    running = jnp.zeros(padded.shape[:-1] + (length,), jnp.float32)
    for offset in range(span):
        running = running + taps[:, offset, :, None].astype(jnp.float32) * padded[..., offset:offset + length].astype(jnp.float32)
    return running

def short_grads(grad_feats, padded_in):
    span = padded_in.shape[-1] - grad_feats.shape[-1] + 1
    length = grad_feats.shape[-1]
    columns = []
    for offset in range(span):
        begin_at = span - 1 - offset
        columns.append(lax.optimization_barrier(jnp.sum(grad_feats.astype(jnp.float32) * padded_in[..., begin_at:begin_at + length].astype(jnp.float32), axis=-1)))
    return jnp.stack(columns, axis=1)

def causal_long(kernel, signal):
    length = signal.shape[1]
    spectra = jnp.fft.rfft(kernel, n=2 * length, axis=1) * jnp.fft.rfft(signal, n=2 * length, axis=1)
    return jnp.fft.irfft(spectra, n=2 * length, axis=1)[:, :length]

def correlate_long(first, second):
    length = second.shape[1]
    spectra = jnp.conj(jnp.fft.rfft(first, n=2 * length, axis=1)) * jnp.fft.rfft(second, n=2 * length, axis=1)
    return jnp.fft.irfft(spectra, n=2 * length, axis=1)[:, :length]

def reference(query_proj, key_proj, value_proj, short_taps, skip_gain, filter_raw, grad_out):
    length = query_proj.shape[1]
    scale_root = 1.0 / math.sqrt(length)
    span = short_taps.shape[1]
    stacked = jnp.stack([query_proj, key_proj, value_proj])
    padded_in = jnp.pad(stacked, ((0, 0), (0, 0), (span - 1, 0)))
    features = short_causal(padded_in, short_taps)
    queries_short = features[0].astype(jnp.bfloat16)
    mixer_in = (features[1] * features[2]).astype(jnp.bfloat16)
    kernel = filter_raw.astype(jnp.float32) * scale_root
    mixer_float = mixer_in.astype(jnp.float32)
    long_out = causal_long(kernel, mixer_float).astype(jnp.bfloat16)
    gate_arg = long_out.astype(jnp.float32) + skip_gain[:, None] * mixer_float
    mixed_out = (queries_short.astype(jnp.float32) * gate_arg).astype(jnp.bfloat16)
    grad_float = grad_out.astype(jnp.float32)
    inner_grad = grad_float * queries_short.astype(jnp.float32)
    grad_query_short = grad_float * gate_arg
    grad_long = inner_grad.astype(jnp.bfloat16).astype(jnp.float32)
    back_mix = correlate_long(kernel, grad_long).astype(jnp.bfloat16)
    grad_filter = (correlate_long(mixer_float, grad_long) * scale_root).astype(jnp.bfloat16)
    grad_mix = (back_mix.astype(jnp.float32) + skip_gain[:, None] * inner_grad).astype(jnp.bfloat16)
    grad_skip = lax.optimization_barrier(jnp.sum(inner_grad * mixer_float, axis=1)) * scale_root
    grad_mix_float = grad_mix.astype(jnp.float32)
    grad_feats = jnp.stack([grad_query_short, grad_mix_float * features[2], grad_mix_float * features[1]]).astype(jnp.bfloat16)
    padded_grad = jnp.pad(grad_feats, ((0, 0), (0, 0), (0, span - 1)))
    grads_in = short_anticausal(padded_grad, short_taps).astype(jnp.bfloat16)
    grad_short = short_grads(grad_feats, padded_in) * scale_root
    return (mixed_out, grads_in[0], grads_in[1], grads_in[2], grad_short, grad_skip, grad_filter)
```

```python
import math

import jax
import jax.numpy as jnp
from jax import lax
from jax.sharding import PartitionSpec as P

def from_behind(value, axis, steps):
    count = lax.axis_size(axis)
    first, last = (max(0, -steps), min(count, count - steps))
    return lax.ppermute(value, axis, [(source, source + steps) for source in range(first, last)])


def short_causal(padded, taps):
    span = taps.shape[1]
    length = padded.shape[-1] - (span - 1)
    running = jnp.zeros(padded.shape[:-1] + (length,), jnp.float32)
    for offset in range(span):
        begin_at = span - 1 - offset
        running = running + taps[:, offset, :, None].astype(jnp.float32) * padded[
            ..., begin_at : begin_at + length
        ].astype(jnp.float32)
    return running


def short_anticausal(padded, taps):
    span = taps.shape[1]
    length = padded.shape[-1] - (span - 1)
    running = jnp.zeros(padded.shape[:-1] + (length,), jnp.float32)
    for offset in range(span):
        running = running + taps[:, offset, :, None].astype(jnp.float32) * padded[
            ..., offset : offset + length
        ].astype(jnp.float32)
    return running


def short_grads(grad_feats, padded_in):
    span = padded_in.shape[-1] - grad_feats.shape[-1] + 1
    length = grad_feats.shape[-1]
    columns = []
    for offset in range(span):
        begin_at = span - 1 - offset
        columns.append(
            jnp.sum(
                grad_feats.astype(jnp.float32)
                * padded_in[..., begin_at : begin_at + length].astype(jnp.float32),
                axis=-1,
            )
        )
    return jnp.stack(columns, axis=1)


def turn_table(rows, columns, period):
    products = (
        lax.broadcasted_iota(jnp.int32, (rows, columns), 0)
        * lax.broadcasted_iota(jnp.int32, (rows, columns), 1)
        % period
    )
    angles = products.astype(jnp.float32) * (2.0 * math.pi / period)
    return (jnp.cos(angles), jnp.sin(angles))


def kept_rows(full_rows):
    return full_rows // 2 + 16


def rounded_product(form, first, second):
    return jnp.einsum(
        form,
        first.astype(jnp.bfloat16),
        second.astype(jnp.bfloat16),
        preferred_element_type=jnp.float32,
    )


def spectrum(signal):
    groups, length = signal.shape
    full_rows = 256
    half_rows = full_rows // 2
    kept = kept_rows(full_rows)
    columns = 2 * length // full_rows
    shaped = signal.reshape(groups, half_rows, columns)
    cos_rows, sin_rows = turn_table(kept, half_rows, full_rows)
    first_re = rounded_product("ca,gab->gcb", cos_rows, shaped)
    first_im = rounded_product("ca,gab->gcb", -sin_rows, shaped)
    cos_twist, sin_twist = turn_table(kept, columns, 2 * length)
    twist_re = first_re * cos_twist + first_im * sin_twist
    twist_im = first_im * cos_twist - first_re * sin_twist
    cos_cols, sin_cols = turn_table(columns, columns, columns)
    out_re = rounded_product("gcb,bd->gcd", twist_re, cos_cols) + rounded_product(
        "gcb,bd->gcd", twist_im, sin_cols
    )
    out_im = rounded_product("gcb,bd->gcd", twist_im, cos_cols) - rounded_product(
        "gcb,bd->gcd", twist_re, sin_cols
    )
    return (out_re.astype(jnp.bfloat16), out_im.astype(jnp.bfloat16))


def inverse_spectrum(spec_re, spec_im):
    groups, kept, columns = spec_re.shape
    full_rows = 256
    spec_re = spec_re.astype(jnp.bfloat16)
    spec_im = spec_im.astype(jnp.bfloat16)
    cos_cols, sin_cols = turn_table(columns, columns, columns)
    back_re = rounded_product("gcd,db->gcb", spec_re, cos_cols) - rounded_product(
        "gcd,db->gcb", spec_im, sin_cols
    )
    back_im = rounded_product("gcd,db->gcb", spec_im, cos_cols) + rounded_product(
        "gcd,db->gcb", spec_re, sin_cols
    )
    cos_twist, sin_twist = turn_table(kept, columns, full_rows * columns)
    twist_re = back_re * cos_twist - back_im * sin_twist
    twist_im = back_im * cos_twist + back_re * sin_twist
    cos_rows, sin_rows = turn_table(kept, full_rows // 2, full_rows)
    row = lax.broadcasted_iota(jnp.int32, (kept, full_rows // 2), 0)
    alone = (row == 0) | (row == full_rows // 2)
    weight = jnp.where(alone, 1.0, jnp.where(row > full_rows // 2, 0.0, 2.0))
    real_part = rounded_product("ca,gcb->gab", cos_rows * weight, twist_re) - rounded_product(
        "ca,gcb->gab", sin_rows * weight, twist_im
    )
    return real_part.reshape(groups, -1) / float(full_rows * columns)


def conj_times(first, second):
    return (
        first[0] * second[0] + first[1] * second[1],
        first[0] * second[1] - first[1] * second[0],
    )


def order_filter(filter_raw, seq_count, chan_count, group_size):
    slab_rows = filter_raw.shape[1]
    return jnp.transpose(
        filter_raw.reshape(chan_count, seq_count, group_size, slab_rows), (1, 0, 2, 3)
    ).reshape(-1, slab_rows)


def restore_filter(returned, seq_count, chan_count, group_size):
    slab_rows = returned.shape[1]
    return jnp.transpose(
        returned.reshape(seq_count, chan_count, group_size, slab_rows), (1, 0, 2, 3)
    ).reshape(-1, slab_rows)


def per_device(query_proj, key_proj, value_proj, short_taps, skip_gain, filter_raw, grad_out):
    channels, steps_local = query_proj.shape
    seq_count = lax.axis_size("seq")
    chan_count = lax.axis_size("chan")
    group_size = channels // seq_count
    length = steps_local * seq_count
    scale_root = 1.0 / math.sqrt(length)
    short_span = short_taps.shape[1]
    stacked = jnp.stack([query_proj, key_proj, value_proj])
    left_rim = from_behind(
        jnp.swapaxes(stacked[:, :, steps_local - (short_span - 1) :], 1, 2), "seq", 1
    )
    padded_in = jnp.concatenate([jnp.swapaxes(left_rim, 1, 2), stacked], axis=2)
    features = short_causal(padded_in, short_taps)
    queries_short = features[0].astype(jnp.bfloat16)
    mixer_in = (features[1] * features[2]).astype(jnp.bfloat16)
    grad_float = grad_out.astype(jnp.float32)
    inner_grad = grad_float * queries_short.astype(jnp.float32)
    grad_long = inner_grad.astype(jnp.bfloat16)
    filter_group = lax.all_to_all(
        order_filter(filter_raw, seq_count, chan_count, group_size),
        ("seq", "chan"),
        split_axis=0,
        concat_axis=1,
        tiled=True,
    )
    filter_group, mixer_sent = lax.optimization_barrier((filter_group, mixer_in))
    mixer_group = lax.all_to_all(mixer_sent, "seq", split_axis=0, concat_axis=1, tiled=True)
    mixer_spec = spectrum(mixer_group)
    raw_spec = spectrum(filter_group)
    mixer_spec = tuple(part.astype(jnp.float32) for part in mixer_spec)
    kernel_spec = tuple(part.astype(jnp.float32) * scale_root for part in raw_spec)
    conv_re = kernel_spec[0] * mixer_spec[0] - kernel_spec[1] * mixer_spec[1]
    conv_im = kernel_spec[0] * mixer_spec[1] + kernel_spec[1] * mixer_spec[0]
    long_group = inverse_spectrum(conv_re, conv_im).astype(jnp.bfloat16)
    long_out = lax.all_to_all(long_group, "seq", split_axis=1, concat_axis=0, tiled=True)
    grad_group = lax.all_to_all(grad_long, "seq", split_axis=0, concat_axis=1, tiled=True)
    grad_spec = tuple(part.astype(jnp.float32) for part in spectrum(grad_group))
    back_group = inverse_spectrum(*conj_times(kernel_spec, grad_spec)).astype(jnp.bfloat16)
    filter_grad_group = (inverse_spectrum(*conj_times(mixer_spec, grad_spec)) * scale_root).astype(
        jnp.bfloat16
    )
    back_mix = lax.all_to_all(back_group, "seq", split_axis=1, concat_axis=0, tiled=True)
    returned = lax.all_to_all(
        filter_grad_group, ("seq", "chan"), split_axis=1, concat_axis=0, tiled=True
    )
    grad_filter = restore_filter(returned, seq_count, chan_count, group_size)
    mixer_float = mixer_in.astype(jnp.float32)
    gate_arg = long_out.astype(jnp.float32) + skip_gain[:, None] * mixer_float
    mixed_out = (queries_short.astype(jnp.float32) * gate_arg).astype(jnp.bfloat16)
    grad_query_short = grad_float * gate_arg
    grad_mix = (back_mix.astype(jnp.float32) + skip_gain[:, None] * inner_grad).astype(jnp.bfloat16)
    skip_part = jnp.sum(inner_grad * mixer_float, axis=1)
    grad_mix_float = grad_mix.astype(jnp.float32)
    grad_feats = jnp.stack(
        [grad_query_short, grad_mix_float * features[2], grad_mix_float * features[1]]
    ).astype(jnp.bfloat16)
    next_feats = from_behind(jnp.swapaxes(grad_feats[:, :, : short_span - 1], 1, 2), "seq", -1)
    padded_grad = jnp.concatenate([grad_feats, jnp.swapaxes(next_feats, 1, 2)], axis=2)
    grads_in = short_anticausal(padded_grad, short_taps).astype(jnp.bfloat16)
    short_part = short_grads(grad_feats, padded_in)
    parts = jnp.concatenate([short_part.reshape(-1, channels), skip_part[None]], axis=0)
    copies = jnp.broadcast_to(parts[None], (seq_count,) + parts.shape)
    sums = jnp.sum(
        lax.all_to_all(copies, "seq", split_axis=0, concat_axis=0, tiled=True), axis=0
    )
    short_sum = sums[:-1].reshape(short_part.shape)
    skip_sum = sums[-1]
    return (
        mixed_out,
        grads_in[0],
        grads_in[1],
        grads_in[2],
        short_sum * scale_root,
        skip_sum * scale_root,
        grad_filter,
    )


def solution(mesh):
    placed = (
        P("chan", "seq"),
        P("chan", "seq"),
        P("chan", "seq"),
        P(None, None, "chan"),
        P("chan"),
        P(None, ("seq", "chan")),
        P("chan", "seq"),
    )
    return jax.shard_map(
        per_device,
        mesh=mesh,
        in_specs=placed,
        out_specs=(
            P("chan", "seq"),
            P("chan", "seq"),
            P("chan", "seq"),
            P("chan", "seq"),
            P(None, None, "chan"),
            P("chan"),
            P(None, ("seq", "chan")),
        ),
        check_vma=False,
    )
```

```python
import math

import jax
import jax.numpy as jnp
from jax import lax
from jax.sharding import PartitionSpec as P

def from_behind(value, axis, steps):
    count = lax.axis_size(axis)
    first, last = (max(0, -steps), min(count, count - steps))
    return lax.ppermute(value, axis, [(source, source + steps) for source in range(first, last)])


def short_causal(padded, taps):
    span = taps.shape[1]
    length = padded.shape[-1] - (span - 1)
    running = jnp.zeros(padded.shape[:-1] + (length,), jnp.float32)
    for offset in range(span):
        begin_at = span - 1 - offset
        running = running + taps[:, offset, :, None].astype(jnp.float32) * padded[
            ..., begin_at : begin_at + length
        ].astype(jnp.float32)
    return running


def short_anticausal(padded, taps):
    span = taps.shape[1]
    length = padded.shape[-1] - (span - 1)
    running = jnp.zeros(padded.shape[:-1] + (length,), jnp.float32)
    for offset in range(span):
        running = running + taps[:, offset, :, None].astype(jnp.float32) * padded[
            ..., offset : offset + length
        ].astype(jnp.float32)
    return running


def short_grads(grad_feats, padded_in):
    span = padded_in.shape[-1] - grad_feats.shape[-1] + 1
    length = grad_feats.shape[-1]
    columns = []
    for offset in range(span):
        begin_at = span - 1 - offset
        columns.append(
            jnp.sum(
                grad_feats.astype(jnp.float32)
                * padded_in[..., begin_at : begin_at + length].astype(jnp.float32),
                axis=-1,
            )
        )
    return jnp.stack(columns, axis=1)


def turn_table(rows, columns, period):
    products = (
        lax.broadcasted_iota(jnp.int32, (rows, columns), 0)
        * lax.broadcasted_iota(jnp.int32, (rows, columns), 1)
        % period
    )
    angles = products.astype(jnp.float32) * (2.0 * math.pi / period)
    return (jnp.cos(angles), jnp.sin(angles))


def kept_rows(full_rows):
    return full_rows // 2 + 16


def rounded_product(form, first, second):
    return jnp.einsum(
        form,
        first.astype(jnp.bfloat16),
        second.astype(jnp.bfloat16),
        preferred_element_type=jnp.float32,
    )


def spectrum(signal):
    groups, length = signal.shape
    full_rows = 256
    half_rows = full_rows // 2
    kept = kept_rows(full_rows)
    columns = 2 * length // full_rows
    shaped = signal.reshape(groups, half_rows, columns)
    cos_rows, sin_rows = turn_table(kept, half_rows, full_rows)
    first_re = rounded_product("ca,gab->gcb", cos_rows, shaped)
    first_im = rounded_product("ca,gab->gcb", -sin_rows, shaped)
    cos_twist, sin_twist = turn_table(kept, columns, 2 * length)
    twist_re = first_re * cos_twist + first_im * sin_twist
    twist_im = first_im * cos_twist - first_re * sin_twist
    cos_cols, sin_cols = turn_table(columns, columns, columns)
    out_re = rounded_product("gcb,bd->gcd", twist_re, cos_cols) + rounded_product(
        "gcb,bd->gcd", twist_im, sin_cols
    )
    out_im = rounded_product("gcb,bd->gcd", twist_im, cos_cols) - rounded_product(
        "gcb,bd->gcd", twist_re, sin_cols
    )
    return (out_re.astype(jnp.bfloat16), out_im.astype(jnp.bfloat16))


def inverse_spectrum(spec_re, spec_im):
    groups, kept, columns = spec_re.shape
    full_rows = 256
    spec_re = spec_re.astype(jnp.bfloat16)
    spec_im = spec_im.astype(jnp.bfloat16)
    cos_cols, sin_cols = turn_table(columns, columns, columns)
    back_re = rounded_product("gcd,db->gcb", spec_re, cos_cols) - rounded_product(
        "gcd,db->gcb", spec_im, sin_cols
    )
    back_im = rounded_product("gcd,db->gcb", spec_im, cos_cols) + rounded_product(
        "gcd,db->gcb", spec_re, sin_cols
    )
    cos_twist, sin_twist = turn_table(kept, columns, full_rows * columns)
    twist_re = back_re * cos_twist - back_im * sin_twist
    twist_im = back_im * cos_twist + back_re * sin_twist
    cos_rows, sin_rows = turn_table(kept, full_rows // 2, full_rows)
    row = lax.broadcasted_iota(jnp.int32, (kept, full_rows // 2), 0)
    alone = (row == 0) | (row == full_rows // 2)
    weight = jnp.where(alone, 1.0, jnp.where(row > full_rows // 2, 0.0, 2.0))
    real_part = rounded_product("ca,gcb->gab", cos_rows * weight, twist_re) - rounded_product(
        "ca,gcb->gab", sin_rows * weight, twist_im
    )
    return real_part.reshape(groups, -1) / float(full_rows * columns)


def conj_times(first, second):
    return (
        first[0] * second[0] + first[1] * second[1],
        first[0] * second[1] - first[1] * second[0],
    )


def order_filter(filter_raw, seq_count, chan_count, group_size):
    slab_rows = filter_raw.shape[1]
    return jnp.transpose(
        filter_raw.reshape(chan_count, seq_count, group_size, slab_rows), (1, 0, 2, 3)
    ).reshape(-1, slab_rows)


def restore_filter(returned, seq_count, chan_count, group_size):
    slab_rows = returned.shape[1]
    return jnp.transpose(
        returned.reshape(seq_count, chan_count, group_size, slab_rows), (1, 0, 2, 3)
    ).reshape(-1, slab_rows)


def per_device(query_proj, key_proj, value_proj, short_taps, skip_gain, filter_raw, grad_out):
    channels, steps_local = query_proj.shape
    seq_count = lax.axis_size("seq")
    chan_count = lax.axis_size("chan")
    group_size = channels // seq_count
    length = steps_local * seq_count
    scale_root = 1.0 / math.sqrt(length)
    short_span = short_taps.shape[1]
    stacked = jnp.stack([query_proj, key_proj, value_proj])
    left_rim = from_behind(
        jnp.swapaxes(stacked[:, :, steps_local - (short_span - 1) :], 1, 2), "seq", 1
    )
    padded_in = jnp.concatenate([jnp.swapaxes(left_rim, 1, 2), stacked], axis=2)
    features = short_causal(padded_in, short_taps)
    queries_short = features[0].astype(jnp.bfloat16)
    mixer_in = (features[1] * features[2]).astype(jnp.bfloat16)
    grad_float = grad_out.astype(jnp.float32)
    inner_grad = grad_float * queries_short.astype(jnp.float32)
    grad_long = inner_grad.astype(jnp.bfloat16)
    filter_group = lax.all_to_all(
        order_filter(filter_raw, seq_count, chan_count, group_size),
        ("seq", "chan"),
        split_axis=0,
        concat_axis=1,
        tiled=True,
    )
    filter_group, mixer_sent = lax.optimization_barrier((filter_group, mixer_in))
    mixer_group = lax.all_to_all(mixer_sent, "seq", split_axis=0, concat_axis=1, tiled=True)
    raw_spec = spectrum(filter_group)
    grad_sent, mixer_group, raw_spec = lax.optimization_barrier((grad_long, mixer_group, raw_spec))
    grad_group = lax.all_to_all(grad_sent, "seq", split_axis=0, concat_axis=1, tiled=True)
    mixer_held = spectrum(mixer_group)
    mixer_spec = tuple(part.astype(jnp.float32) for part in mixer_held)
    kernel_spec = tuple(part.astype(jnp.float32) * scale_root for part in raw_spec)
    conv_re = kernel_spec[0] * mixer_spec[0] - kernel_spec[1] * mixer_spec[1]
    conv_im = kernel_spec[0] * mixer_spec[1] + kernel_spec[1] * mixer_spec[0]
    long_group = inverse_spectrum(conv_re, conv_im).astype(jnp.bfloat16)
    grad_group, long_group = lax.optimization_barrier((grad_group, long_group))
    long_out = lax.all_to_all(long_group, "seq", split_axis=1, concat_axis=0, tiled=True)
    grad_held = spectrum(grad_group)
    grad_spec = tuple(part.astype(jnp.float32) for part in grad_held)
    back_group = inverse_spectrum(*conj_times(kernel_spec, grad_spec)).astype(jnp.bfloat16)
    grad_held, back_group = lax.optimization_barrier((grad_held, back_group))
    back_mix = lax.all_to_all(back_group, "seq", split_axis=1, concat_axis=0, tiled=True)
    grad_spec = tuple(part.astype(jnp.float32) for part in grad_held)
    filter_grad_group = (inverse_spectrum(*conj_times(mixer_spec, grad_spec)) * scale_root).astype(
        jnp.bfloat16
    )
    returned = lax.all_to_all(
        filter_grad_group, ("seq", "chan"), split_axis=1, concat_axis=0, tiled=True
    )
    grad_filter = restore_filter(returned, seq_count, chan_count, group_size)
    mixer_float = mixer_in.astype(jnp.float32)
    gate_arg = long_out.astype(jnp.float32) + skip_gain[:, None] * mixer_float
    mixed_out = (queries_short.astype(jnp.float32) * gate_arg).astype(jnp.bfloat16)
    grad_query_short = grad_float * gate_arg
    grad_mix = (back_mix.astype(jnp.float32) + skip_gain[:, None] * inner_grad).astype(jnp.bfloat16)
    skip_part = jnp.sum(inner_grad * mixer_float, axis=1)
    grad_mix_float = grad_mix.astype(jnp.float32)
    grad_feats = jnp.stack(
        [grad_query_short, grad_mix_float * features[2], grad_mix_float * features[1]]
    ).astype(jnp.bfloat16)
    next_feats = from_behind(jnp.swapaxes(grad_feats[:, :, : short_span - 1], 1, 2), "seq", -1)
    padded_grad = jnp.concatenate([grad_feats, jnp.swapaxes(next_feats, 1, 2)], axis=2)
    grads_in = short_anticausal(padded_grad, short_taps).astype(jnp.bfloat16)
    short_part = short_grads(grad_feats, padded_in)
    parts = jnp.concatenate([short_part.reshape(-1, channels), skip_part[None]], axis=0)
    copies = jnp.broadcast_to(parts[None], (seq_count,) + parts.shape)
    sums = jnp.sum(
        lax.all_to_all(copies, "seq", split_axis=0, concat_axis=0, tiled=True), axis=0
    )
    short_sum = sums[:-1].reshape(short_part.shape)
    skip_sum = sums[-1]
    return (
        mixed_out,
        grads_in[0],
        grads_in[1],
        grads_in[2],
        short_sum * scale_root,
        skip_sum * scale_root,
        grad_filter,
    )


def solution(mesh):
    placed = (
        P("chan", "seq"),
        P("chan", "seq"),
        P("chan", "seq"),
        P(None, None, "chan"),
        P("chan"),
        P(None, ("seq", "chan")),
        P("chan", "seq"),
    )
    return jax.shard_map(
        per_device,
        mesh=mesh,
        in_specs=placed,
        out_specs=(
            P("chan", "seq"),
            P("chan", "seq"),
            P("chan", "seq"),
            P("chan", "seq"),
            P(None, None, "chan"),
            P("chan"),
            P(None, ("seq", "chan")),
        ),
        check_vma=False,
    )
```

```python
import math

import jax
import jax.numpy as jnp
from jax import lax
from jax.sharding import PartitionSpec as P

def from_behind(value, axis, steps):
    count = lax.axis_size(axis)
    first, last = (max(0, -steps), min(count, count - steps))
    return lax.ppermute(value, axis, [(source, source + steps) for source in range(first, last)])


def short_causal(padded, taps):
    span = taps.shape[1]
    length = padded.shape[-1] - (span - 1)
    running = jnp.zeros(padded.shape[:-1] + (length,), jnp.float32)
    for offset in range(span):
        begin_at = span - 1 - offset
        running = running + taps[:, offset, :, None].astype(jnp.float32) * padded[
            ..., begin_at : begin_at + length
        ].astype(jnp.float32)
    return running


def short_anticausal(padded, taps):
    span = taps.shape[1]
    length = padded.shape[-1] - (span - 1)
    running = jnp.zeros(padded.shape[:-1] + (length,), jnp.float32)
    for offset in range(span):
        running = running + taps[:, offset, :, None].astype(jnp.float32) * padded[
            ..., offset : offset + length
        ].astype(jnp.float32)
    return running


def short_grads(grad_feats, padded_in):
    span = padded_in.shape[-1] - grad_feats.shape[-1] + 1
    length = grad_feats.shape[-1]
    columns = []
    for offset in range(span):
        begin_at = span - 1 - offset
        columns.append(
            jnp.sum(
                grad_feats.astype(jnp.float32)
                * padded_in[..., begin_at : begin_at + length].astype(jnp.float32),
                axis=-1,
            )
        )
    return jnp.stack(columns, axis=1)


def turn_table(rows, columns, period):
    products = (
        lax.broadcasted_iota(jnp.int32, (rows, columns), 0)
        * lax.broadcasted_iota(jnp.int32, (rows, columns), 1)
        % period
    )
    angles = products.astype(jnp.float32) * (2.0 * math.pi / period)
    return (jnp.cos(angles), jnp.sin(angles))


def kept_rows(full_rows):
    return full_rows // 2 + 16


def rounded_product(form, first, second):
    return jnp.einsum(
        form,
        first.astype(jnp.bfloat16),
        second.astype(jnp.bfloat16),
        preferred_element_type=jnp.float32,
    )


def spectrum(signal):
    groups, length = signal.shape
    full_rows = 256
    half_rows = full_rows // 2
    kept = kept_rows(full_rows)
    columns = 2 * length // full_rows
    shaped = signal.reshape(groups, half_rows, columns)
    cos_rows, sin_rows = turn_table(kept, half_rows, full_rows)
    first_re = rounded_product("ca,gab->gcb", cos_rows, shaped)
    first_im = rounded_product("ca,gab->gcb", -sin_rows, shaped)
    cos_twist, sin_twist = turn_table(kept, columns, 2 * length)
    twist_re = first_re * cos_twist + first_im * sin_twist
    twist_im = first_im * cos_twist - first_re * sin_twist
    cos_cols, sin_cols = turn_table(columns, columns, columns)
    out_re = rounded_product("gcb,bd->gcd", twist_re, cos_cols) + rounded_product(
        "gcb,bd->gcd", twist_im, sin_cols
    )
    out_im = rounded_product("gcb,bd->gcd", twist_im, cos_cols) - rounded_product(
        "gcb,bd->gcd", twist_re, sin_cols
    )
    return (out_re.astype(jnp.bfloat16), out_im.astype(jnp.bfloat16))


def inverse_spectrum(spec_re, spec_im):
    groups, kept, columns = spec_re.shape
    full_rows = 256
    spec_re = spec_re.astype(jnp.bfloat16)
    spec_im = spec_im.astype(jnp.bfloat16)
    cos_cols, sin_cols = turn_table(columns, columns, columns)
    back_re = rounded_product("gcd,db->gcb", spec_re, cos_cols) - rounded_product(
        "gcd,db->gcb", spec_im, sin_cols
    )
    back_im = rounded_product("gcd,db->gcb", spec_im, cos_cols) + rounded_product(
        "gcd,db->gcb", spec_re, sin_cols
    )
    cos_twist, sin_twist = turn_table(kept, columns, full_rows * columns)
    twist_re = back_re * cos_twist - back_im * sin_twist
    twist_im = back_im * cos_twist + back_re * sin_twist
    cos_rows, sin_rows = turn_table(kept, full_rows // 2, full_rows)
    row = lax.broadcasted_iota(jnp.int32, (kept, full_rows // 2), 0)
    alone = (row == 0) | (row == full_rows // 2)
    weight = jnp.where(alone, 1.0, jnp.where(row > full_rows // 2, 0.0, 2.0))
    real_part = rounded_product("ca,gcb->gab", cos_rows * weight, twist_re) - rounded_product(
        "ca,gcb->gab", sin_rows * weight, twist_im
    )
    return real_part.reshape(groups, -1) / float(full_rows * columns)


def conj_times(first, second):
    return (
        first[0] * second[0] + first[1] * second[1],
        first[0] * second[1] - first[1] * second[0],
    )


def order_filter(filter_raw, seq_count, chan_count, group_size):
    slab_rows = filter_raw.shape[1]
    return jnp.transpose(
        filter_raw.reshape(chan_count, seq_count, group_size, slab_rows), (1, 0, 2, 3)
    ).reshape(-1, slab_rows)


def restore_filter(returned, seq_count, chan_count, group_size):
    slab_rows = returned.shape[1]
    return jnp.transpose(
        returned.reshape(seq_count, chan_count, group_size, slab_rows), (1, 0, 2, 3)
    ).reshape(-1, slab_rows)


def per_device(query_proj, key_proj, value_proj, short_taps, skip_gain, filter_raw, grad_out):
    channels, steps_local = query_proj.shape
    seq_count = lax.axis_size("seq")
    chan_count = lax.axis_size("chan")
    group_size = channels // seq_count
    length = steps_local * seq_count
    scale_root = 1.0 / math.sqrt(length)
    short_span = short_taps.shape[1]
    stacked = jnp.stack([query_proj, key_proj, value_proj])
    rim = jnp.stack(
        [
            stream[:, steps_local - (short_span - 1) :]
            for stream in (query_proj, key_proj, value_proj)
        ]
    )
    left_rim = from_behind(jnp.swapaxes(rim, 1, 2), "seq", 1)
    filter_sent = order_filter(filter_raw, seq_count, chan_count, group_size)
    left_rim, filter_sent = lax.optimization_barrier((left_rim, filter_sent))
    padded_in = jnp.concatenate([jnp.swapaxes(left_rim, 1, 2), stacked], axis=2)
    features = short_causal(padded_in, short_taps)
    queries_short = features[0].astype(jnp.bfloat16)
    mixer_in = (features[1] * features[2]).astype(jnp.bfloat16)
    grad_float = grad_out.astype(jnp.float32)
    inner_grad = grad_float * queries_short.astype(jnp.float32)
    grad_long = inner_grad.astype(jnp.bfloat16)
    filter_group = lax.all_to_all(
        filter_sent,
        ("seq", "chan"),
        split_axis=0,
        concat_axis=1,
        tiled=True,
    )
    filter_group, mixer_sent = lax.optimization_barrier((filter_group, mixer_in))
    mixer_group = lax.all_to_all(mixer_sent, "seq", split_axis=0, concat_axis=1, tiled=True)
    raw_spec = spectrum(filter_group)
    grad_sent, mixer_group, raw_spec = lax.optimization_barrier((grad_long, mixer_group, raw_spec))
    grad_group = lax.all_to_all(grad_sent, "seq", split_axis=0, concat_axis=1, tiled=True)
    mixer_held = spectrum(mixer_group)
    mixer_spec = tuple(part.astype(jnp.float32) for part in mixer_held)
    kernel_spec = tuple(part.astype(jnp.float32) * scale_root for part in raw_spec)
    conv_re = kernel_spec[0] * mixer_spec[0] - kernel_spec[1] * mixer_spec[1]
    conv_im = kernel_spec[0] * mixer_spec[1] + kernel_spec[1] * mixer_spec[0]
    long_group = inverse_spectrum(conv_re, conv_im).astype(jnp.bfloat16)
    grad_group, long_group = lax.optimization_barrier((grad_group, long_group))
    long_out = lax.all_to_all(long_group, "seq", split_axis=1, concat_axis=0, tiled=True)
    grad_held = spectrum(grad_group)
    grad_spec = tuple(part.astype(jnp.float32) for part in grad_held)
    back_group = inverse_spectrum(*conj_times(kernel_spec, grad_spec)).astype(jnp.bfloat16)
    grad_held, back_group = lax.optimization_barrier((grad_held, back_group))
    back_mix = lax.all_to_all(back_group, "seq", split_axis=1, concat_axis=0, tiled=True)
    grad_spec = tuple(part.astype(jnp.float32) for part in grad_held)
    filter_grad_group = (inverse_spectrum(*conj_times(mixer_spec, grad_spec)) * scale_root).astype(
        jnp.bfloat16
    )
    returned = lax.all_to_all(
        filter_grad_group, ("seq", "chan"), split_axis=1, concat_axis=0, tiled=True
    )
    grad_filter = restore_filter(returned, seq_count, chan_count, group_size)
    mixer_float = mixer_in.astype(jnp.float32)
    gate_arg = long_out.astype(jnp.float32) + skip_gain[:, None] * mixer_float
    mixed_out = (queries_short.astype(jnp.float32) * gate_arg).astype(jnp.bfloat16)
    grad_query_short = grad_float * gate_arg
    grad_mix = (back_mix.astype(jnp.float32) + skip_gain[:, None] * inner_grad).astype(jnp.bfloat16)
    skip_part = jnp.sum(inner_grad * mixer_float, axis=1)
    grad_mix_float = grad_mix.astype(jnp.float32)
    grad_feats = jnp.stack(
        [grad_query_short, grad_mix_float * features[2], grad_mix_float * features[1]]
    ).astype(jnp.bfloat16)
    next_feats = from_behind(jnp.swapaxes(grad_feats[:, :, : short_span - 1], 1, 2), "seq", -1)
    padded_grad = jnp.concatenate([grad_feats, jnp.swapaxes(next_feats, 1, 2)], axis=2)
    grads_in = [
        short_anticausal(padded_grad[at : at + 1], short_taps[at : at + 1])[0].astype(jnp.bfloat16)
        for at in range(3)
    ]
    short_part = short_grads(grad_feats, padded_in)
    parts = jnp.concatenate([short_part.reshape(-1, channels), skip_part[None]], axis=0)
    copies = jnp.broadcast_to(parts[None], (seq_count,) + parts.shape)
    sums = jnp.sum(
        lax.all_to_all(copies, "seq", split_axis=0, concat_axis=0, tiled=True), axis=0
    )
    short_sum = sums[:-1].reshape(short_part.shape)
    skip_sum = sums[-1]
    return (
        mixed_out,
        grads_in[0],
        grads_in[1],
        grads_in[2],
        short_sum * scale_root,
        skip_sum * scale_root,
        grad_filter,
    )


def solution(mesh):
    placed = (
        P("chan", "seq"),
        P("chan", "seq"),
        P("chan", "seq"),
        P(None, None, "chan"),
        P("chan"),
        P(None, ("seq", "chan")),
        P("chan", "seq"),
    )
    return jax.shard_map(
        per_device,
        mesh=mesh,
        in_specs=placed,
        out_specs=(
            P("chan", "seq"),
            P("chan", "seq"),
            P("chan", "seq"),
            P("chan", "seq"),
            P(None, None, "chan"),
            P("chan"),
            P(None, ("seq", "chan")),
        ),
        check_vma=False,
    )
```

```python
import math

import jax
import jax.numpy as jnp
from jax import lax
from jax.sharding import PartitionSpec as P

def from_behind(value, axis, steps):
    count = lax.axis_size(axis)
    first, last = (max(0, -steps), min(count, count - steps))
    return lax.ppermute(value, axis, [(source, source + steps) for source in range(first, last)])


def short_causal(padded, taps):
    span = taps.shape[1]
    length = padded.shape[-1] - (span - 1)
    running = jnp.zeros(padded.shape[:-1] + (length,), jnp.float32)
    for offset in range(span):
        begin_at = span - 1 - offset
        running = running + taps[:, offset, :, None].astype(jnp.float32) * padded[
            ..., begin_at : begin_at + length
        ].astype(jnp.float32)
    return running


def short_anticausal(padded, taps):
    span = taps.shape[1]
    length = padded.shape[-1] - (span - 1)
    running = jnp.zeros(padded.shape[:-1] + (length,), jnp.float32)
    for offset in range(span):
        running = running + taps[:, offset, :, None].astype(jnp.float32) * padded[
            ..., offset : offset + length
        ].astype(jnp.float32)
    return running


def short_grads(grad_feats, padded_in):
    span = padded_in.shape[-1] - grad_feats.shape[-1] + 1
    length = grad_feats.shape[-1]
    columns = []
    for offset in range(span):
        begin_at = span - 1 - offset
        columns.append(
            jnp.sum(
                grad_feats.astype(jnp.float32)
                * padded_in[..., begin_at : begin_at + length].astype(jnp.float32),
                axis=-1,
            )
        )
    return jnp.stack(columns, axis=1)


def turn_table(rows, columns, period):
    products = (
        lax.broadcasted_iota(jnp.int32, (rows, columns), 0)
        * lax.broadcasted_iota(jnp.int32, (rows, columns), 1)
        % period
    )
    angles = products.astype(jnp.float32) * (2.0 * math.pi / period)
    return (jnp.cos(angles), jnp.sin(angles))


def kept_rows(full_rows):
    return full_rows // 2 + 16


def rounded_product(form, first, second):
    return jnp.einsum(
        form,
        first.astype(jnp.bfloat16),
        second.astype(jnp.bfloat16),
        preferred_element_type=jnp.float32,
    )


def spectrum(signal):
    groups, length = signal.shape
    full_rows = 256
    half_rows = full_rows // 2
    kept = kept_rows(full_rows)
    columns = 2 * length // full_rows
    shaped = signal.reshape(groups, half_rows, columns)
    cos_rows, sin_rows = turn_table(kept, half_rows, full_rows)
    first_re = rounded_product("ca,gab->gcb", cos_rows, shaped)
    first_im = rounded_product("ca,gab->gcb", -sin_rows, shaped)
    cos_twist, sin_twist = turn_table(kept, columns, 2 * length)
    twist_re = first_re * cos_twist + first_im * sin_twist
    twist_im = first_im * cos_twist - first_re * sin_twist
    cos_cols, sin_cols = turn_table(columns, columns, columns)
    out_re = rounded_product("gcb,bd->gcd", twist_re, cos_cols) + rounded_product(
        "gcb,bd->gcd", twist_im, sin_cols
    )
    out_im = rounded_product("gcb,bd->gcd", twist_im, cos_cols) - rounded_product(
        "gcb,bd->gcd", twist_re, sin_cols
    )
    return (out_re.astype(jnp.bfloat16), out_im.astype(jnp.bfloat16))


def inverse_spectrum(spec_re, spec_im):
    groups, kept, columns = spec_re.shape
    full_rows = 256
    spec_re = spec_re.astype(jnp.bfloat16)
    spec_im = spec_im.astype(jnp.bfloat16)
    cos_cols, sin_cols = turn_table(columns, columns, columns)
    back_re = rounded_product("gcd,db->gcb", spec_re, cos_cols) - rounded_product(
        "gcd,db->gcb", spec_im, sin_cols
    )
    back_im = rounded_product("gcd,db->gcb", spec_im, cos_cols) + rounded_product(
        "gcd,db->gcb", spec_re, sin_cols
    )
    cos_twist, sin_twist = turn_table(kept, columns, full_rows * columns)
    twist_re = back_re * cos_twist - back_im * sin_twist
    twist_im = back_im * cos_twist + back_re * sin_twist
    cos_rows, sin_rows = turn_table(kept, full_rows // 2, full_rows)
    row = lax.broadcasted_iota(jnp.int32, (kept, full_rows // 2), 0)
    alone = (row == 0) | (row == full_rows // 2)
    weight = jnp.where(alone, 1.0, jnp.where(row > full_rows // 2, 0.0, 2.0))
    real_part = rounded_product("ca,gcb->gab", cos_rows * weight, twist_re) - rounded_product(
        "ca,gcb->gab", sin_rows * weight, twist_im
    )
    return real_part.reshape(groups, -1) / float(full_rows * columns)


def conj_times(first, second):
    return (
        first[0] * second[0] + first[1] * second[1],
        first[0] * second[1] - first[1] * second[0],
    )


def order_filter(filter_raw, seq_count, chan_count, group_size):
    slab_rows = filter_raw.shape[1]
    return jnp.transpose(
        filter_raw.reshape(chan_count, seq_count, group_size, slab_rows), (1, 0, 2, 3)
    ).reshape(-1, slab_rows)


def restore_filter(returned, seq_count, chan_count, group_size):
    slab_rows = returned.shape[1]
    return jnp.transpose(
        returned.reshape(seq_count, chan_count, group_size, slab_rows), (1, 0, 2, 3)
    ).reshape(-1, slab_rows)


def per_device(query_proj, key_proj, value_proj, short_taps, skip_gain, filter_raw, grad_out):
    channels, steps_local = query_proj.shape
    seq_count = lax.axis_size("seq")
    chan_count = lax.axis_size("chan")
    group_size = channels // seq_count
    length = steps_local * seq_count
    scale_root = 1.0 / math.sqrt(length)
    short_span = short_taps.shape[1]
    stacked = jnp.stack([query_proj, key_proj, value_proj])
    rim = jnp.stack(
        [
            stream[:, steps_local - (short_span - 1) :]
            for stream in (query_proj, key_proj, value_proj)
        ]
    )
    left_rim = from_behind(jnp.swapaxes(rim, 1, 2), "seq", 1)
    filter_sent = order_filter(filter_raw, seq_count, chan_count, group_size)
    left_rim, filter_sent = lax.optimization_barrier((left_rim, filter_sent))
    padded_in = jnp.concatenate([jnp.swapaxes(left_rim, 1, 2), stacked], axis=2)
    features = [
        short_causal(padded_in[at : at + 1], short_taps[at : at + 1])[0] for at in range(3)
    ]
    queries_short = features[0].astype(jnp.bfloat16)
    mixer_in = (features[1] * features[2]).astype(jnp.bfloat16)
    grad_float = grad_out.astype(jnp.float32)
    inner_grad = grad_float * queries_short.astype(jnp.float32)
    grad_long = inner_grad.astype(jnp.bfloat16)
    filter_group = lax.all_to_all(
        filter_sent,
        ("seq", "chan"),
        split_axis=0,
        concat_axis=1,
        tiled=True,
    )
    filter_group, mixer_sent = lax.optimization_barrier((filter_group, mixer_in))
    mixer_group = lax.all_to_all(mixer_sent, "seq", split_axis=0, concat_axis=1, tiled=True)
    raw_spec = spectrum(filter_group)
    grad_sent, mixer_group, raw_spec = lax.optimization_barrier((grad_long, mixer_group, raw_spec))
    grad_group = lax.all_to_all(grad_sent, "seq", split_axis=0, concat_axis=1, tiled=True)
    mixer_held = spectrum(mixer_group)
    mixer_spec = tuple(part.astype(jnp.float32) for part in mixer_held)
    kernel_spec = tuple(part.astype(jnp.float32) * scale_root for part in raw_spec)
    conv_re = kernel_spec[0] * mixer_spec[0] - kernel_spec[1] * mixer_spec[1]
    conv_im = kernel_spec[0] * mixer_spec[1] + kernel_spec[1] * mixer_spec[0]
    long_group = inverse_spectrum(conv_re, conv_im).astype(jnp.bfloat16)
    grad_group, long_group = lax.optimization_barrier((grad_group, long_group))
    long_out = lax.all_to_all(long_group, "seq", split_axis=1, concat_axis=0, tiled=True)
    grad_held = spectrum(grad_group)
    grad_spec = tuple(part.astype(jnp.float32) for part in grad_held)
    back_group = inverse_spectrum(*conj_times(kernel_spec, grad_spec)).astype(jnp.bfloat16)
    grad_held, back_group = lax.optimization_barrier((grad_held, back_group))
    back_mix = lax.all_to_all(back_group, "seq", split_axis=1, concat_axis=0, tiled=True)
    grad_spec = tuple(part.astype(jnp.float32) for part in grad_held)
    filter_grad_group = (inverse_spectrum(*conj_times(mixer_spec, grad_spec)) * scale_root).astype(
        jnp.bfloat16
    )
    returned = lax.all_to_all(
        filter_grad_group, ("seq", "chan"), split_axis=1, concat_axis=0, tiled=True
    )
    grad_filter = restore_filter(returned, seq_count, chan_count, group_size)
    mixer_float = mixer_in.astype(jnp.float32)
    gate_arg = long_out.astype(jnp.float32) + skip_gain[:, None] * mixer_float
    mixed_out = (queries_short.astype(jnp.float32) * gate_arg).astype(jnp.bfloat16)
    grad_query_short = grad_float * gate_arg
    grad_mix = (back_mix.astype(jnp.float32) + skip_gain[:, None] * inner_grad).astype(jnp.bfloat16)
    skip_part = jnp.sum(inner_grad * mixer_float, axis=1)
    grad_mix_float = grad_mix.astype(jnp.float32)
    grad_feats = jnp.stack(
        [grad_query_short, grad_mix_float * features[2], grad_mix_float * features[1]]
    ).astype(jnp.bfloat16)
    next_feats = from_behind(jnp.swapaxes(grad_feats[:, :, : short_span - 1], 1, 2), "seq", -1)
    padded_grad = jnp.concatenate([grad_feats, jnp.swapaxes(next_feats, 1, 2)], axis=2)
    grads_in = [
        short_anticausal(padded_grad[at : at + 1], short_taps[at : at + 1])[0].astype(jnp.bfloat16)
        for at in range(3)
    ]
    short_part = short_grads(grad_feats, padded_in)
    parts = jnp.concatenate([short_part.reshape(-1, channels), skip_part[None]], axis=0)
    copies = jnp.broadcast_to(parts[None], (seq_count,) + parts.shape)
    sums = jnp.sum(
        lax.all_to_all(copies, "seq", split_axis=0, concat_axis=0, tiled=True), axis=0
    )
    short_sum = sums[:-1].reshape(short_part.shape)
    skip_sum = sums[-1]
    return (
        mixed_out,
        grads_in[0],
        grads_in[1],
        grads_in[2],
        short_sum * scale_root,
        skip_sum * scale_root,
        grad_filter,
    )


def solution(mesh):
    placed = (
        P("chan", "seq"),
        P("chan", "seq"),
        P("chan", "seq"),
        P(None, None, "chan"),
        P("chan"),
        P(None, ("seq", "chan")),
        P("chan", "seq"),
    )
    return jax.shard_map(
        per_device,
        mesh=mesh,
        in_specs=placed,
        out_specs=(
            P("chan", "seq"),
            P("chan", "seq"),
            P("chan", "seq"),
            P("chan", "seq"),
            P(None, None, "chan"),
            P("chan"),
            P(None, ("seq", "chan")),
        ),
        check_vma=False,
    )
```
